256 devices in a mesh: dp: 4 (over x), ctx: 64 (over z, y, core).
Axes of the slice: x: 4, y: 4, z: 8, core: 2. Of those that a mesh axis runs over, the one named last changes fastest.
Arguments:
- queries: bfloat16 [2, 32768, 2048], P(None, ('dp', 'ctx')), may hold values from -6 to 6
- keys: bfloat16 [2, 32768, 1024], P(None, ('dp', 'ctx')), may hold values from -6 to 6
- values: bfloat16 [2, 32768, 1024], P(None, ('dp', 'ctx')), may hold values from -6 to 6
- doc_start: int32 [2, 32768], P(None, ('dp', 'ctx')), may hold values from 0 to 16383, as said below
- gain_q: float32 [128], replicated, may hold values from 0.5 to 1.5
- key_norm_gain: float32 [128], replicated, may hold values from 0.5 to 1.5
- cotangent: bfloat16 [2, 32768, 2048], P(None, ('dp', 'ctx')), may hold values from -6 to 6
Outputs:
- attended: bfloat16 [2, 32768, 2048], P(None, ('dp', 'ctx'))
- grad_queries: bfloat16 [2, 32768, 2048], P(None, ('dp', 'ctx'))
- grad_keys: bfloat16 [2, 32768, 1024], P(None, ('dp', 'ctx'))
- value_gradients: bfloat16 [2, 32768, 1024], P(None, ('dp', 'ctx'))
- grad_gain_q: float32 [128], replicated
- grad_gain_k: float32 [128], replicated
The draws below stay inside these ranges and needn't reach their ends.
Inputs may be any that keep to these rules, and one draw needn't show every extreme that they name: doc_start gives each token the position in its sequence of its document's first token; the documents of a sequence are runs of 1 to 256 tokens, the first starting at 0, and every sequence has one of exactly 256 tokens.
All inputs are finite; a program needn't handle non-finite values.
Results may differ from the reference program's by a relative error of at most 0.012.
Values may be sent and summed in bfloat16 or wider, within the bound.
No kernel may reach another device: no remote copies, remote signals or barrier semaphores. Data moves between devices by JAX's collectives and lax.ppermute only.
A program may use at most 128 MiB of HBM per device.

```python
import jax
import jax.numpy as jnp
from jax import lax

BLK = 128
HQ = 16
KEY_VALUE_HEADS = 8
HEAD_SIZE = 128
L = 16384
MOST = 256
SEQS = 4
HALF_ROWS = 32768


def draw_doc_start(key, part):
    lengths = jax.random.randint(jax.random.fold_in(key, 11), (SEQS, L), 1, MOST + 1)
    chosen = jax.random.randint(jax.random.fold_in(key, 12), (SEQS, 1), 0, 2)
    counter = jnp.arange(L, dtype=jnp.int32)
    lengths = jnp.where(counter[None, :] == chosen, MOST, lengths).astype(jnp.int32)
    starts = jnp.cumsum(lengths, axis=1) - lengths
    located = jax.vmap(lambda row: jnp.searchsorted(row, counter, side='right'))(starts) - 1
    first = jnp.take_along_axis(starts, located.astype(jnp.int32), axis=1)
    middle = L // 2
    lower = first[:, :middle].reshape(-1)
    upper = first[:, middle:][:, ::-1].reshape(-1)
    return jnp.stack([lower, upper]).astype(jnp.int32)


def levels(rng, dims, split, smallest, top_value):
    level, own = 1.0, jax.random.fold_in(rng, 6)
    for dim, parts in split:
        draws = jnp.exp(jax.random.uniform(jax.random.fold_in(own, dim), (parts,), jnp.float32, smallest / len(split), top_value / len(split)))
        level = level * jnp.repeat(draws, dims[dim] // parts).reshape([-1 if axis == dim else 1 for axis in range(len(dims))])
    return level


def bell_draw(own_key, dims, spread, limit, pieces=(), kind=jnp.bfloat16):
    drawn = spread * jax.random.normal(own_key, dims, jnp.float32)
    if pieces:
        drawn = drawn * levels(own_key, dims, pieces, -0.22, 0.18)
    return jnp.clip(drawn, -limit, limit).astype(kind)


def setup_inputs(seed: int = 0) -> dict:
    streams_of = jax.random.split(jax.random.key(seed), 8)
    queries = bell_draw(streams_of[0], (2, HALF_ROWS, HQ * HEAD_SIZE), 1.0, 6.0, ((1, 256),))
    keys = bell_draw(streams_of[1], (2, HALF_ROWS, KEY_VALUE_HEADS * HEAD_SIZE), 1.0, 6.0, ((1, 256),))
    values = bell_draw(streams_of[2], (2, HALF_ROWS, KEY_VALUE_HEADS * HEAD_SIZE), 1.0, 6.0, ((1, 256),))
    doc_start = draw_doc_start(jax.random.fold_in(streams_of[7], 71), 0)
    gain_q = jnp.clip(1.0 + 0.1 * jax.random.normal(streams_of[4], (HEAD_SIZE,), jnp.float32), 0.5, 1.5)
    key_norm_gain = jnp.clip(1.0 + 0.1 * jax.random.normal(streams_of[5], (HEAD_SIZE,), jnp.float32), 0.5, 1.5)
    cotangent = bell_draw(streams_of[6], (2, HALF_ROWS, HQ * HEAD_SIZE), 1.0, 6.0, ((1, 256),))
    return {"queries": queries, "keys": keys, "values": values, "doc_start": doc_start, "gain_q": gain_q, "key_norm_gain": key_norm_gain, "cotangent": cotangent}


query_factor = 168.0 ** (-0.5)
rotary_base = 1000000.0
norm_epsilon = 1e-06

def rotary_angles(position, head_width):
    exponent = jnp.arange(head_width // 2, dtype=jnp.float32) * (2.0 / head_width)
    frequency = jnp.exp(-exponent * jnp.log(jnp.float32(rotary_base)))
    return position.astype(jnp.float32)[..., None] * frequency

def prepare(tensor, gain, angle, factor):
    inverse = lax.rsqrt(lax.optimization_barrier(jnp.mean(tensor * tensor, axis=-1, keepdims=True)) + norm_epsilon)
    normed = tensor * inverse * gain
    middle = tensor.shape[-1] // 2
    cosine = jnp.cos(angle)[..., None, :]
    sine = jnp.sin(angle)[..., None, :]
    first = normed[..., :middle]
    second = normed[..., middle:]
    return jnp.concatenate([first * cosine - second * sine, second * cosine + first * sine], axis=-1) * factor

def to_natural(stored_array):
    middle = L // 2
    lower = stored_array[0].reshape((SEQS, middle) + stored_array.shape[2:])
    upper = stored_array[1].reshape((SEQS, middle) + stored_array.shape[2:])[:, ::-1]
    return jnp.concatenate([lower, upper], axis=1)

def to_stored(natural_array):
    middle = L // 2
    lower = natural_array[:, :middle].reshape((SEQS * middle,) + natural_array.shape[2:])
    upper = natural_array[:, middle:][:, ::-1].reshape((SEQS * middle,) + natural_array.shape[2:])
    return jnp.stack([lower, upper])

def rounded(tensor):
    return lax.optimization_barrier(tensor.astype(jnp.bfloat16)).astype(jnp.float32)

def product(form, left, right):
    return jnp.einsum(form, left.astype(jnp.float32), right.astype(jnp.float32), precision=lax.Precision.HIGHEST)

def one_sequence(operands, gain_q, key_norm_gain):
    queries, keys, values, doc_start, cotangent = operands
    head_width = gain_q.shape[0]
    q_heads = queries.shape[1] // head_width
    kv_heads = keys.shape[1] // head_width
    repeat = q_heads // kv_heads
    position = jnp.arange(L, dtype=jnp.int32)
    angle = rotary_angles(position, head_width)
    q_rotated, q_back = jax.vjp(lambda tensor, gain: prepare(tensor, gain, angle, query_factor), queries.astype(jnp.float32).reshape(L, q_heads, head_width), gain_q)
    q_rot = q_rotated.astype(jnp.bfloat16).reshape(L, kv_heads, repeat, head_width)
    k_rotated, k_back = jax.vjp(lambda tensor, gain: prepare(tensor, gain, angle, 1.0), keys.astype(jnp.float32).reshape(L, kv_heads, head_width), key_norm_gain)
    k_rot = k_rotated.astype(jnp.bfloat16)
    v_heads = values.reshape(L, kv_heads, head_width)
    cotangent_heads = cotangent.reshape(L, kv_heads, repeat, head_width)
    padding = MOST
    k_pad = jnp.concatenate([jnp.zeros((padding, kv_heads, head_width), k_rot.dtype), k_rot])
    v_pad = jnp.concatenate([jnp.zeros((padding, kv_heads, head_width), v_heads.dtype), v_heads])
    key_position = jnp.concatenate([jnp.full((padding,), -1, jnp.int32), position])
    width = 2 * BLK
    window = padding + width

    def block_step(carry, index):
        grad_k_pad, grad_v_pad = carry
        start = (index * width).astype(jnp.int32)
        q_block = lax.dynamic_slice_in_dim(q_rot, start, width, 0)
        cotangent_block = lax.dynamic_slice_in_dim(cotangent_heads, start, width, 0)
        doc_block = lax.dynamic_slice_in_dim(doc_start, start, width, 0)
        query_position = lax.dynamic_slice_in_dim(position, start, width, 0)
        k_block = lax.dynamic_slice_in_dim(k_pad, start, window, 0)
        v_block = lax.dynamic_slice_in_dim(v_pad, start, window, 0)
        seen_position = lax.dynamic_slice_in_dim(key_position, start, window, 0)
        mask = (doc_block[:, None] <= seen_position[None, :]) & (seen_position[None, :] <= query_position[:, None])
        scores = product('ihrd,jhd->hrij', q_block, k_block)
        expo = jnp.where(mask[None, None], jnp.exp(scores), 0.0)
        total = lax.optimization_barrier(jnp.sum(expo, axis=-1))
        mixed = product('hrij,jhd->ihrd', rounded(expo), v_block)
        attended_block = lax.optimization_barrier((mixed / jnp.transpose(total, (2, 0, 1))[..., None]).astype(jnp.bfloat16))
        delta = product('ihrd,ihrd->hri', cotangent_block, attended_block)
        probs = jnp.where(mask[None, None], jnp.exp(scores) / total[..., None], 0.0)
        dprob = product('ihrd,jhd->hrij', cotangent_block, v_block)
        dscore = probs * (dprob - delta[..., None])
        probs_round = rounded(probs)
        dscore_round = rounded(dscore)
        grad_q_block = product('hrij,jhd->ihrd', dscore_round, k_block)
        grad_k_window = product('hrij,ihrd->jhd', dscore_round, q_block)
        grad_v_window = product('hrij,ihrd->jhd', probs_round, cotangent_block)
        grad_k_pad = lax.dynamic_update_slice_in_dim(grad_k_pad, lax.dynamic_slice_in_dim(grad_k_pad, start, window, 0) + grad_k_window, start, 0)
        grad_v_pad = lax.dynamic_update_slice_in_dim(grad_v_pad, lax.dynamic_slice_in_dim(grad_v_pad, start, window, 0) + grad_v_window, start, 0)
        return ((grad_k_pad, grad_v_pad), (attended_block, grad_q_block))
    initial = (jnp.zeros((padding + L, kv_heads, head_width), jnp.float32), jnp.zeros((padding + L, kv_heads, head_width), jnp.float32))
    finals, blocks = lax.scan(block_step, initial, jnp.arange(L // width, dtype=jnp.int32))
    grad_k_pad, grad_v_pad = finals
    attended_blocks, query_block_gradients = blocks
    attended = attended_blocks.reshape(L, q_heads * head_width)
    grad_queries, grad_gain_q = q_back(query_block_gradients.reshape(L, q_heads, head_width))
    grad_keys, grad_gain_k = k_back(grad_k_pad[padding:])
    return (attended, grad_queries.astype(jnp.bfloat16).reshape(L, q_heads * head_width), grad_keys.astype(jnp.bfloat16).reshape(L, kv_heads * head_width), grad_v_pad[padding:].astype(jnp.bfloat16).reshape(L, kv_heads * head_width), grad_gain_q, grad_gain_k)

def reference(queries, keys, values, doc_start, gain_q, key_norm_gain, cotangent):
    operands = (to_natural(queries), to_natural(keys), to_natural(values), to_natural(doc_start), to_natural(cotangent))
    results = lax.map(lambda item: one_sequence(item, gain_q, key_norm_gain), operands)
    attended, grad_queries, grad_keys, value_gradients, gains_q, gains_k = results
    return (to_stored(attended), to_stored(grad_queries), to_stored(grad_keys), to_stored(value_gradients), lax.optimization_barrier(jnp.sum(gains_q, axis=0)), lax.optimization_barrier(jnp.sum(gains_k, axis=0)))
```

```python
import functools

import jax
import jax.numpy as jnp
from jax import lax
from jax.experimental import pallas as pl
from jax.experimental.pallas import tpu as pltpu
from jax.sharding import PartitionSpec as P

query_factor = 168.0 ** (-0.5)
rotary_base = 1000000.0
norm_epsilon = 1e-06
PANELS = 3
F32 = jnp.float32
BF16 = jnp.bfloat16


def rotary_angles(position, head_width):
    exponent = jnp.arange(head_width // 2, dtype=F32) * (2.0 / head_width)
    frequency = jnp.exp(-exponent * jnp.log(F32(rotary_base)))
    return position.astype(F32)[..., None] * frequency


def slot_positions(slot, rows, group, block):
    ascending = slot * block + rows
    descending = slot * block + block - 1 - rows
    inside = (slot >= 0) & (slot < 2 * group)
    return jnp.where(inside, jnp.where(slot < group, ascending, descending), -1)


def half_turn(x):
    return pltpu.roll(x, x.shape[-1] // 2, 1)


def normalize(x):
    inverse = lax.rsqrt(jnp.mean(x * x, axis=-1, keepdims=True) + norm_epsilon)
    return x * inverse, inverse


def rotate(y, cosine, sine):
    return y * cosine + half_turn(y) * sine


def unrotate(g, cosine, sine):
    return g * cosine + half_turn(g * sine)


def norm_back(grad, normed, inverse):
    return inverse * (grad - normed * jnp.mean(grad * normed, axis=-1, keepdims=True))


def contract(a, b, da, db):
    return lax.dot_general(a, b, (((da,), (db,)), ((), ())), preferred_element_type=F32)


def attend_kernel(
    group,
    index_ref,
    doc_ref,
    gain_q_ref,
    gain_k_ref,
    cos_ref,
    sin_ref,
    q_ref,
    k_ref,
    v_ref,
    c_ref,
    lo1_ref,
    hi1_ref,
    lo2_ref,
    hi2_ref,
    att_ref,
    gq_ref,
    own_k_ref,
    own_v_ref,
    lo1_out,
    hi1_out,
    lo2_out,
    hi2_out,
    gains_ref,
    mask_ref,
):
    step = pl.program_id(0)
    block = q_ref.shape[1]
    width = k_ref.shape[2]
    repeat = q_ref.shape[2] // width
    device = index_ref[0]

    @pl.when(step == 0)
    def _():
        gains_ref[...] = jnp.zeros_like(gains_ref)
        for x in range(2):
            slot = device if x == 0 else 2 * group - 1 - device
            lane = lax.broadcasted_iota(jnp.int32, (block, block), 1)
            row = lax.broadcasted_iota(jnp.int32, (block, block), 0)
            query_position = slot * block + (lane if x == 0 else block - 1 - lane)
            for panel in range(PANELS):
                seen = slot - panel
                upward = seen < group
                key_position = (
                    seen * block
                    + jnp.where(upward, 0, block - 1)
                    + jnp.where(upward, 1, -1) * row
                )
                key_position = jnp.where(seen >= 0, key_position, -1)
                allowed = (doc_ref[x : x + 1, :] <= key_position) & (key_position <= query_position)
                value = jnp.where(allowed, 1.0, 0.0).astype(F32)
                for r in range(repeat):
                    mask_ref[
                        x, panel * block : (panel + 1) * block, r * block : (r + 1) * block
                    ] = value

    gain_q = gain_q_ref[...] * query_factor
    gain_k = gain_k_ref[...]
    near = (lo1_ref, hi1_ref)
    far = (lo2_ref, hi2_ref)
    near_out = (lo1_out, hi1_out)
    far_out = (lo2_out, hi2_out)
    sum_q = jnp.zeros((1, width), F32)
    sum_k = jnp.zeros((1, width), F32)
    for x in range(2):
        cos_q = cos_ref[x, 0]
        sin_q = sin_ref[x, 0]
        q_parts, q_normed, q_inverse, c_parts = [], [], [], []
        for r in range(repeat):
            normed, inverse = normalize(q_ref[x, :, r * width : (r + 1) * width].astype(F32))
            q_normed.append(normed)
            q_inverse.append(inverse)
            q_parts.append(rotate(normed * gain_q, cos_q, sin_q).astype(BF16))
            c_parts.append(c_ref[x, :, r * width : (r + 1) * width])
        q_rot = jnp.concatenate(q_parts, axis=0)
        cot = jnp.concatenate(c_parts, axis=0)
        raw_k = (k_ref[x], near[x][0], far[x][0])
        k_parts, k_normed, k_inverse = [], [], []
        for panel in range(PANELS):
            normed, inverse = normalize(raw_k[panel].astype(F32))
            k_normed.append(normed)
            k_inverse.append(inverse)
            k_parts.append(
                rotate(normed * gain_k, cos_ref[x, panel], sin_ref[x, panel]).astype(BF16)
            )
        k_rot = jnp.concatenate(k_parts, axis=0)
        vals = jnp.concatenate([v_ref[x], near[x][1], far[x][1]], axis=0)
        expo = jnp.exp(contract(k_rot, q_rot, 1, 1)) * mask_ref[x]
        dprob = contract(vals, cot, 1, 1)
        inverse_total = 1.0 / jnp.sum(expo, axis=0, keepdims=True)
        probs = expo * inverse_total
        delta = jnp.sum(probs * dprob, axis=0, keepdims=True)
        dscore = (probs * (dprob - delta)).astype(BF16)
        probs = probs.astype(BF16)
        attended = contract(probs, vals, 0, 0)
        grad_q = contract(dscore, k_rot, 0, 0)
        grad_v = contract(probs, cot, 1, 0)
        grad_k = contract(dscore, q_rot, 1, 0)
        for r in range(repeat):
            rows = slice(r * block, (r + 1) * block)
            cols = slice(r * width, (r + 1) * width)
            att_ref[x, :, cols] = attended[rows].astype(BF16)
            back = unrotate(grad_q[rows], cos_q, sin_q)
            sum_q = sum_q + jnp.sum(back * q_normed[r], axis=0, keepdims=True)
            gq_ref[x, :, cols] = norm_back(back * gain_q, q_normed[r], q_inverse[r]).astype(BF16)
        for panel in range(PANELS):
            rows = slice(panel * block, (panel + 1) * block)
            back = unrotate(grad_k[rows], cos_ref[x, panel], sin_ref[x, panel])
            sum_k = sum_k + jnp.sum(back * k_normed[panel], axis=0, keepdims=True)
            raw = norm_back(back * gain_k, k_normed[panel], k_inverse[panel])
            if panel == 0:
                own_k_ref[x] = raw
                own_v_ref[x] = grad_v[rows]
            else:
                target = near_out[x] if panel == 1 else far_out[x]
                target[0] = raw.astype(BF16)
                target[1] = grad_v[rows].astype(BF16)
    gains_ref[0:1, :] += sum_q * query_factor
    gains_ref[1:2, :] += sum_k


def attend(group, device, doc_start, gain_q, gain_k, cosine, sine, queries, keys, values, cotangent, panels):
    block = queries.shape[1]
    width = gain_q.shape[0]
    heads = keys.shape[2] // width
    repeat = queries.shape[2] // keys.shape[2]
    whole = lambda shape: pl.BlockSpec(shape, lambda h: (0,) * len(shape))
    wide = pl.BlockSpec((2, block, repeat * width), lambda h: (0, 0, h))
    slim = pl.BlockSpec((2, block, width), lambda h: (0, 0, h))
    pair = jax.ShapeDtypeStruct((2, block, heads * width), BF16)
    pairs = 2 * heads * block * repeat * block * PANELS * width
    return pl.pallas_call(
        functools.partial(attend_kernel, group),
        grid=(heads,),
        in_specs=[
            pl.BlockSpec(memory_space=pltpu.SMEM),
            whole((2, block)),
            whole((1, width)),
            whole((1, width)),
            whole((2, PANELS, block, width)),
            whole((2, PANELS, block, width)),
            wide,
            slim,
            slim,
            wide,
            slim,
            slim,
            slim,
            slim,
        ],
        out_specs=[wide, wide, slim, slim, slim, slim, slim, slim, whole((2, width))],
        out_shape=[
            jax.ShapeDtypeStruct(queries.shape, BF16),
            jax.ShapeDtypeStruct(queries.shape, BF16),
            jax.ShapeDtypeStruct(keys.shape, F32),
            jax.ShapeDtypeStruct(keys.shape, F32),
            pair,
            pair,
            pair,
            pair,
            jax.ShapeDtypeStruct((2, width), F32),
        ],
        scratch_shapes=[pltpu.VMEM((2, PANELS * block, repeat * block), F32)],
        compiler_params=pltpu.CompilerParams(
            dimension_semantics=("arbitrary",), vmem_limit_bytes=40 * 1024 * 1024
        ),
        cost_estimate=pl.CostEstimate(
            flops=12 * pairs, bytes_accessed=12 * 1024 * 1024, transcendentals=pairs // width
        ),
        name="attend",
    )(device, doc_start, gain_q[None], gain_k[None], cosine, sine, queries, keys, values, cotangent, *panels)


def total_over(x, axis):
    size = lax.axis_size(axis)
    distance = 1
    while distance < size:
        x = x + lax.ppermute(x, axis, [(i, i ^ distance) for i in range(size)])
        distance *= 2
    return x


def shards(queries, keys, values, doc_start, gain_q, key_norm_gain, cotangent):
    group = lax.axis_size("ctx")
    block = queries.shape[1]
    width = gain_q.shape[0]
    device = lax.axis_index("ctx")
    at_fold = device == group - 1
    upward = [(i, i + 1) for i in range(group - 1)]
    downward = [(i + 1, i) for i in range(group - 1)]
    up = lambda a: lax.ppermute(a, "ctx", upward)
    down = lambda a: lax.ppermute(a, "ctx", downward)

    low = jnp.stack([keys[0], values[0]])
    high = jnp.stack([keys[1], values[1]])
    low1 = up(low)
    high1 = jnp.where(at_fold, low, down(high))
    low2 = up(low1)
    high2 = down(high1)
    high2 = jnp.where(at_fold, low1, high2)

    rows = jnp.arange(block, dtype=jnp.int32)
    slots = jnp.stack([device, 2 * group - 1 - device])[:, None] - jnp.arange(PANELS)[None, :]
    angle = rotary_angles(slot_positions(slots[..., None], rows, group, block), width)
    cosine = jnp.cos(angle)
    sine = jnp.sin(angle)
    cosine = jnp.concatenate([cosine, cosine], axis=-1)
    sine = jnp.concatenate([-sine, sine], axis=-1)

    attended, grad_queries, own_k, own_v, low1_g, high1_g, low2_g, high2_g, gains = attend(
        group,
        device[None].astype(jnp.int32),
        doc_start,
        gain_q,
        key_norm_gain,
        cosine,
        sine,
        queries,
        keys,
        values,
        cotangent,
        (low1, high1, low2, high2),
    )
    back_low = jnp.where(at_fold, high2_g, down(low2_g))
    back_high = up(high2_g)
    back_low = (back_low.astype(F32) + low1_g.astype(F32)).astype(BF16)
    back_high = (back_high.astype(F32) + high1_g.astype(F32)).astype(BF16)
    home_low = jnp.where(at_fold, back_high, down(back_low))
    home_high = up(back_high)
    gains = total_over(total_over(gains, "ctx"), "dp")
    home = jnp.stack([home_low, home_high], axis=1).astype(F32)
    grad_keys = (own_k + home[0]).astype(BF16)
    grad_values = (own_v + home[1]).astype(BF16)
    return attended, grad_queries, grad_keys, grad_values, gains[0], gains[1]


def solution(mesh):
    tokens = P(None, ("dp", "ctx"), None)
    return jax.shard_map(
        shards,
        mesh=mesh,
        in_specs=(tokens, tokens, tokens, P(None, ("dp", "ctx")), P(), P(), tokens),
        out_specs=(tokens, tokens, tokens, tokens, P(), P()),
        check_vma=False,
    )
```

```python
import functools

import jax
import jax.numpy as jnp
from jax import lax
from jax.experimental import pallas as pl
from jax.experimental.pallas import tpu as pltpu
from jax.sharding import PartitionSpec as P

query_factor = 168.0 ** (-0.5)
rotary_base = 1000000.0
norm_epsilon = 1e-06
PANELS = 3
F32 = jnp.float32
BF16 = jnp.bfloat16


def rotary_angles(position, head_width):
    exponent = jnp.arange(head_width // 2, dtype=F32) * (2.0 / head_width)
    frequency = jnp.exp(-exponent * jnp.log(F32(rotary_base)))
    return position.astype(F32)[..., None] * frequency


def slot_positions(slot, rows, group, block):
    ascending = slot * block + rows
    descending = slot * block + block - 1 - rows
    inside = (slot >= 0) & (slot < 2 * group)
    return jnp.where(inside, jnp.where(slot < group, ascending, descending), -1)


def half_turn(x):
    return pltpu.roll(x, x.shape[-1] // 2, 1)


def lane_sum(x, terms):
    width = x.shape[-1]
    parts = []
    for _ in range(terms):
        parts.append(x.astype(BF16))
        x = x - parts[-1].astype(F32)
    split = jnp.concatenate(parts, axis=-1)
    return contract(split, jnp.ones((terms * width, width), BF16), 1, 0)


def normalize(x):
    inverse = lax.rsqrt(lane_sum(x * x, 2) * (1.0 / x.shape[-1]) + norm_epsilon)
    return x * inverse, inverse


def rotate(raw, inverse, gain, cosine, sine):
    turned = half_turn(raw).astype(F32)
    return inverse * (raw.astype(F32) * (gain * cosine) + turned * (half_turn(gain) * sine))


def unrotate(g, cosine, sine):
    return g * cosine + half_turn(g * sine)


def norm_back(grad, normed, inverse):
    return inverse * (grad - normed * (lane_sum(grad * normed, 1) * (1.0 / grad.shape[-1])))


def contract(a, b, da, db):
    return lax.dot_general(a, b, (((da,), (db,)), ((), ())), preferred_element_type=F32)


def attend_kernel(
    group,
    index_ref,
    doc_ref,
    gain_q_ref,
    gain_k_ref,
    cos_ref,
    sin_ref,
    q_ref,
    k_ref,
    v_ref,
    c_ref,
    pair_ref,
    cross_ref,
    skip_ref,
    relay_ref,
    att_ref,
    gq_ref,
    own_k_ref,
    own_v_ref,
    near_pair_out,
    near_cross_out,
    far_pair_out,
    far_cross_out,
    gains_ref,
    mask_ref,
):
    step = pl.program_id(0)
    block = q_ref.shape[1]
    width = k_ref.shape[2]
    repeat = q_ref.shape[2] // width
    device = index_ref[0]

    @pl.when(step == 0)
    def _():
        gains_ref[...] = jnp.zeros_like(gains_ref)
        for x in range(2):
            slot = device if x == 0 else 2 * group - 1 - device
            lane = lax.broadcasted_iota(jnp.int32, (block, block), 1)
            row = lax.broadcasted_iota(jnp.int32, (block, block), 0)
            query_position = slot * block + (lane if x == 0 else block - 1 - lane)
            for panel in range(PANELS):
                seen = slot - panel
                upward = seen < group
                key_position = (
                    seen * block
                    + jnp.where(upward, 0, block - 1)
                    + jnp.where(upward, 1, -1) * row
                )
                key_position = jnp.where(seen >= 0, key_position, -1)
                allowed = (doc_ref[x : x + 1, :] <= key_position) & (key_position <= query_position)
                value = jnp.where(allowed, 1.0, 0.0).astype(F32)
                for r in range(repeat):
                    mask_ref[
                        x, panel * block : (panel + 1) * block, r * block : (r + 1) * block
                    ] = value

    gain_q = jnp.broadcast_to(gain_q_ref[...] * query_factor, (block, width))
    gain_k = jnp.broadcast_to(gain_k_ref[...], (block, width))
    even = device % 2 == 0
    at_fold = device == group - 1
    near, far = [], []
    for part, own_ref in ((0, k_ref), (1, v_ref)):
        from_pair, from_cross = pair_ref[part], cross_ref[part]
        from_skip, from_relay = skip_ref[part], relay_ref[part]
        high_near = jnp.where(even, from_pair, jnp.where(at_fold, own_ref[0], from_cross))
        high_far = jnp.where(even, from_relay, jnp.where(at_fold, from_pair, from_skip))
        near.append((jnp.where(even, from_cross, from_pair), high_near))
        far.append((jnp.where(even, from_skip, from_relay), high_far))
    near_grad, far_grad = [], []
    sum_q = jnp.zeros((1, width), F32)
    sum_k = jnp.zeros((1, width), F32)
    for x in range(2):
        cos_q = cos_ref[x, 0]
        sin_q = sin_ref[x, 0]
        q_parts, q_normed, q_inverse, c_parts = [], [], [], []
        for r in range(repeat):
            normed, inverse = normalize(q_ref[x, :, r * width : (r + 1) * width].astype(F32))
            q_normed.append(normed)
            q_inverse.append(inverse)
            q_parts.append(rotate(q_ref[x, :, r * width : (r + 1) * width], inverse, gain_q, cos_q, sin_q).astype(BF16))
            c_parts.append(c_ref[x, :, r * width : (r + 1) * width])
        q_rot = jnp.concatenate(q_parts, axis=0)
        cot = jnp.concatenate(c_parts, axis=0)
        raw_k = (k_ref[x], near[0][x], far[0][x])
        k_parts, k_normed, k_inverse = [], [], []
        for panel in range(PANELS):
            normed, inverse = normalize(raw_k[panel].astype(F32))
            k_normed.append(normed)
            k_inverse.append(inverse)
            k_parts.append(
                rotate(raw_k[panel], inverse, gain_k, cos_ref[x, panel], sin_ref[x, panel]).astype(BF16)
            )
        k_rot = jnp.concatenate(k_parts, axis=0)
        vals = jnp.concatenate([v_ref[x], near[1][x], far[1][x]], axis=0)
        expo = jnp.exp(contract(k_rot, q_rot, 1, 1)) * mask_ref[x]
        dprob = contract(vals, cot, 1, 1)
        inverse_total = 1.0 / jnp.sum(expo, axis=0, keepdims=True)
        probs = expo * inverse_total
        delta = jnp.sum(probs * dprob, axis=0, keepdims=True)
        dscore = (probs * (dprob - delta)).astype(BF16)
        probs = probs.astype(BF16)
        attended = contract(probs, vals, 0, 0)
        grad_q = contract(dscore, k_rot, 0, 0)
        grad_v = contract(probs, cot, 1, 0)
        grad_k = contract(dscore, q_rot, 1, 0)
        for r in range(repeat):
            rows = slice(r * block, (r + 1) * block)
            cols = slice(r * width, (r + 1) * width)
            att_ref[x, :, cols] = attended[rows].astype(BF16)
            back = unrotate(grad_q[rows], cos_q, sin_q)
            sum_q = sum_q + jnp.sum(back * q_normed[r], axis=0, keepdims=True)
            gq_ref[x, :, cols] = norm_back(back * gain_q, q_normed[r], q_inverse[r]).astype(BF16)
        for panel in range(PANELS):
            rows = slice(panel * block, (panel + 1) * block)
            back = unrotate(grad_k[rows], cos_ref[x, panel], sin_ref[x, panel])
            sum_k = sum_k + jnp.sum(back * k_normed[panel], axis=0, keepdims=True)
            raw = norm_back(back * gain_k, k_normed[panel], k_inverse[panel])
            if panel == 0:
                own_k_ref[x] = raw
                own_v_ref[x] = grad_v[rows]
            else:
                target = near_grad if panel == 1 else far_grad
                target.append((raw, grad_v[rows]))
    for part in range(2):
        low, high = near_grad[0][part], near_grad[1][part]
        low_far, high_far = far_grad[0][part], far_grad[1][part]
        joined = jnp.where(at_fold, low + high_far, low)
        near_pair_out[part] = jnp.where(even, high, joined).astype(BF16)
        near_cross_out[part] = jnp.where(even, low, high).astype(BF16)
        far_pair_out[part] = jnp.where(even, high_far, low_far).astype(BF16)
        far_cross_out[part] = jnp.where(even, low_far, high_far).astype(BF16)
    gains_ref[0:1, :] += sum_q * query_factor
    gains_ref[1:2, :] += sum_k


def attend(group, device, doc_start, gain_q, gain_k, cosine, sine, queries, keys, values, cotangent, panels):
    block = queries.shape[1]
    width = gain_q.shape[0]
    heads = keys.shape[2] // width
    repeat = queries.shape[2] // keys.shape[2]
    whole = lambda shape: pl.BlockSpec(shape, lambda h: (0,) * len(shape))
    wide = pl.BlockSpec((2, block, repeat * width), lambda h: (0, 0, h))
    slim = pl.BlockSpec((2, block, width), lambda h: (0, 0, h))
    pair = jax.ShapeDtypeStruct((2, block, heads * width), BF16)
    pairs = 2 * heads * block * repeat * block * PANELS * width
    return pl.pallas_call(
        functools.partial(attend_kernel, group),
        grid=(heads,),
        in_specs=[
            pl.BlockSpec(memory_space=pltpu.SMEM),
            whole((2, block)),
            whole((1, width)),
            whole((1, width)),
            whole((2, PANELS, block, width)),
            whole((2, PANELS, block, width)),
            wide,
            slim,
            slim,
            wide,
            slim,
            slim,
            slim,
            slim,
        ],
        out_specs=[wide, wide, slim, slim, slim, slim, slim, slim, whole((2, width))],
        out_shape=[
            jax.ShapeDtypeStruct(queries.shape, BF16),
            jax.ShapeDtypeStruct(queries.shape, BF16),
            jax.ShapeDtypeStruct(keys.shape, F32),
            jax.ShapeDtypeStruct(keys.shape, F32),
            pair,
            pair,
            pair,
            pair,
            jax.ShapeDtypeStruct((2, width), F32),
        ],
        scratch_shapes=[pltpu.VMEM((2, PANELS * block, repeat * block), F32)],
        compiler_params=pltpu.CompilerParams(
            dimension_semantics=("arbitrary",), vmem_limit_bytes=40 * 1024 * 1024
        ),
        cost_estimate=pl.CostEstimate(
            flops=12 * pairs, bytes_accessed=12 * 1024 * 1024, transcendentals=pairs // width
        ),
        name="attend",
    )(device, doc_start, gain_q[None], gain_k[None], cosine, sine, queries, keys, values, cotangent, *panels)


def gather_kernel(group, index_ref, own_k_ref, own_v_ref, pair_ref, skip_ref, cross_ref, pay_ref, gk_ref, gv_ref):
    device = index_ref[0]
    even = device % 2 == 0
    at_fold = device == group - 1
    for part, own_ref, out_ref in ((0, own_k_ref, gk_ref), (1, own_v_ref, gv_ref)):
        direct = pair_ref[part].astype(F32) + skip_ref[part].astype(F32)
        across = cross_ref[part].astype(F32) + jnp.where(at_fold, pay_ref[part].astype(F32), 0.0)
        out_ref[0] = (own_ref[0] + jnp.where(even, direct, across)).astype(BF16)
        out_ref[1] = (own_ref[1] + jnp.where(even, across, direct)).astype(BF16)


def gather(group, device, own_k, own_v, *arrived):
    _, block, columns = own_k.shape
    tile = 256
    spec = pl.BlockSpec((2, block, tile), lambda h: (0, 0, h))
    return pl.pallas_call(
        functools.partial(gather_kernel, group),
        grid=(columns // tile,),
        in_specs=[pl.BlockSpec(memory_space=pltpu.SMEM)] + [spec] * 6,
        out_specs=[spec, spec],
        out_shape=[jax.ShapeDtypeStruct(own_k.shape, BF16)] * 2,
        compiler_params=pltpu.CompilerParams(dimension_semantics=("arbitrary",)),
        cost_estimate=pl.CostEstimate(
            flops=8 * own_k.size, bytes_accessed=16 * own_k.size, transcendentals=0
        ),
        name="gather",
    )(device, own_k, own_v, *arrived)


def move(x, pairs):
    return lax.ppermute(x, "ctx", pairs)


def total_over(x, axis, first, last):
    size = lax.axis_size(axis)
    distance = first
    while distance < last:
        x = x + lax.ppermute(x, axis, [(i, i ^ distance) for i in range(size)])
        distance *= 2
    return x


def shards(queries, keys, values, doc_start, gain_q, key_norm_gain, cotangent):
    group = lax.axis_size("ctx")
    block = queries.shape[1]
    width = gain_q.shape[0]
    device = lax.axis_index("ctx")
    index = device[None].astype(jnp.int32)
    even = device % 2 == 0
    at_fold = device == group - 1
    evens = range(0, group, 2)
    pairs = [(i, i ^ 1) for i in range(group)]
    cross = [(i + 1, i + 2) for i in evens if i + 2 < group]
    cross = cross + [(b, a) for a, b in cross]
    skip_in = [(i, i + 2) for i in evens if i + 2 < group]
    skip_in = skip_in + [(i + 3, i + 1) for i in evens if i + 3 < group]
    skip_out = [(b, a) for a, b in skip_in]

    low = jnp.stack([keys[0], values[0]])
    high = jnp.stack([keys[1], values[1]])
    first = jnp.where(even, low, high)
    second = jnp.where(even, high, low)
    from_cross = move(second, cross)
    from_skip = move(first, skip_in)
    from_pair = move(first, pairs)
    from_relay = move(jnp.where(at_fold, second, from_cross), pairs)

    rows = jnp.arange(block, dtype=jnp.int32)
    slots = jnp.stack([device, 2 * group - 1 - device])[:, None] - jnp.arange(PANELS)[None, :]
    angle = rotary_angles(slot_positions(slots[..., None], rows, group, block), width)
    cosine = jnp.cos(angle)
    sine = jnp.sin(angle)
    cosine = jnp.concatenate([cosine, cosine], axis=-1)
    sine = jnp.concatenate([-sine, sine], axis=-1)

    attended, grad_queries, own_k, own_v, near_pair, near_cross, far_pair, far_cross, gains = attend(
        group,
        index,
        doc_start,
        gain_q,
        key_norm_gain,
        cosine,
        sine,
        queries,
        keys,
        values,
        cotangent,
        (from_pair, from_cross, from_skip, from_relay),
    )
    back_relay = move(far_pair, pairs)
    back_pair = move(near_pair, pairs)
    back_skip = move(far_cross, skip_out)
    pay = (near_cross.astype(F32) + back_relay.astype(F32)).astype(BF16)
    back_cross = move(pay, cross)
    everyone = lax.axis_size("ctx") * lax.axis_size("dp")
    spread = jnp.broadcast_to(gains[None], (everyone,) + gains.shape)
    gains = jnp.sum(lax.all_to_all(spread, ("dp", "ctx"), 0, 0, tiled=True), axis=0)
    grad_keys, grad_values = gather(group, index, own_k, own_v, back_pair, back_skip, back_cross, pay)
    return attended, grad_queries, grad_keys, grad_values, gains[0], gains[1]


def solution(mesh):
    tokens = P(None, ("dp", "ctx"), None)
    return jax.shard_map(
        shards,
        mesh=mesh,
        in_specs=(tokens, tokens, tokens, P(None, ("dp", "ctx")), P(), P(), tokens),
        out_specs=(tokens, tokens, tokens, tokens, P(), P()),
        check_vma=False,
    )
```

```python
import functools

import jax
import jax.numpy as jnp
from jax import lax
from jax.experimental import pallas as pl
from jax.experimental.pallas import tpu as pltpu
from jax.sharding import PartitionSpec as P

query_factor = 168.0 ** (-0.5)
rotary_base = 1000000.0
norm_epsilon = 1e-06
PANELS = 3
F32 = jnp.float32
BF16 = jnp.bfloat16


def rotary_angles(position, head_width):
    exponent = jnp.arange(head_width // 2, dtype=F32) * (2.0 / head_width)
    frequency = jnp.exp(-exponent * jnp.log(F32(rotary_base)))
    return position.astype(F32)[..., None] * frequency


def slot_positions(slot, rows, group, block):
    ascending = slot * block + rows
    descending = slot * block + block - 1 - rows
    inside = (slot >= 0) & (slot < 2 * group)
    return jnp.where(inside, jnp.where(slot < group, ascending, descending), -1)


def half_turn(x):
    return pltpu.roll(x, x.shape[-1] // 2, 1)


def lane_sum(x, terms):
    width = x.shape[-1]
    parts = []
    for _ in range(terms):
        parts.append(x.astype(BF16))
        x = x - parts[-1].astype(F32)
    split = jnp.concatenate(parts, axis=-1)
    return contract(split, jnp.ones((terms * width, width), BF16), 1, 0)


def normalize(x):
    inverse = lax.rsqrt(lane_sum(x * x, 2) * (1.0 / x.shape[-1]) + norm_epsilon)
    return x * inverse, inverse


def rotate(raw, inverse, gain, cosine, sine):
    turned = half_turn(raw).astype(F32)
    return inverse * (raw.astype(F32) * (gain * cosine) + turned * (half_turn(gain) * sine))


def unrotate(g, cosine, sine):
    return g * cosine + half_turn(g * sine)


def norm_back(grad, normed, inverse):
    return inverse * (grad - normed * (lane_sum(grad * normed, 1) * (1.0 / grad.shape[-1])))


def contract(a, b, da, db):
    return lax.dot_general(a, b, (((da,), (db,)), ((), ())), preferred_element_type=F32)


def in_hbm(x):
    return pltpu.with_memory_space_constraint(x, pltpu.HBM)


def prepare_kernel(gain_q_ref, gain_k_ref, cos_ref, sin_ref, q_ref, k_ref, qr_ref, qi_ref, kr_ref, ki_ref):
    width = gain_q_ref.shape[1]
    jobs = []
    for x in range(2):
        jobs.append((x, k_ref, kr_ref, ki_ref, slice(0, width), gain_k_ref[...]))
        for r in range(q_ref.shape[2] // width):
            cols = slice(r * width, (r + 1) * width)
            jobs.append((x, q_ref, qr_ref, qi_ref, cols, gain_q_ref[...] * query_factor))
    norms = [normalize(src[x, :, cols].astype(F32))[1] for x, src, _, _, cols, _ in jobs]
    for inverse, (x, src, out, inv_out, cols, gain) in zip(norms, jobs):
        gain = jnp.broadcast_to(gain, inverse.shape)
        turned = rotate(src[x, :, cols], inverse, gain, cos_ref[x], sin_ref[x])
        out[x, :, cols] = turned.astype(BF16)
        inv_out[x, :, cols] = inverse


def prepare(gain_q, gain_k, cosine, sine, queries, keys):
    _, block, columns = keys.shape
    width = gain_q.shape[0]
    repeat = queries.shape[2] // columns
    whole = lambda shape: pl.BlockSpec(shape, lambda h: (0,) * len(shape))
    wide = pl.BlockSpec((2, block, repeat * width), lambda h: (0, 0, h))
    slim = pl.BlockSpec((2, block, width), lambda h: (0, 0, h))
    return pl.pallas_call(
        prepare_kernel,
        grid=(columns // width,),
        in_specs=[
            whole((1, width)),
            whole((1, width)),
            whole((2, block, width)),
            whole((2, block, width)),
            wide,
            slim,
        ],
        out_specs=[wide, wide, slim, slim],
        out_shape=[
            pltpu.HBM(queries.shape, BF16),
            pltpu.HBM(queries.shape, F32),
            pltpu.HBM(keys.shape, BF16),
            pltpu.HBM(keys.shape, F32),
        ],
        compiler_params=pltpu.CompilerParams(dimension_semantics=("arbitrary",)),
        cost_estimate=pl.CostEstimate(
            flops=64 * queries.size, bytes_accessed=16 * queries.size, transcendentals=queries.size
        ),
        name="prepare",
    )(gain_q[None], gain_k[None], cosine, sine, in_hbm(queries), in_hbm(keys))


def attend_kernel(
    group,
    index_ref,
    doc_ref,
    gain_q_ref,
    gain_k_ref,
    cos_ref,
    sin_ref,
    q_ref,
    k_ref,
    v_ref,
    c_ref,
    pair_ref,
    cross_ref,
    skip_ref,
    relay_ref,
    qr_ref,
    qi_ref,
    kr_ref,
    ki_ref,
    att_ref,
    gq_ref,
    own_k_ref,
    own_v_ref,
    near_pair_out,
    near_cross_out,
    far_pair_out,
    far_cross_out,
    gains_ref,
    mask_ref,
):
    step = pl.program_id(0)
    block = q_ref.shape[1]
    width = k_ref.shape[2]
    repeat = q_ref.shape[2] // width
    device = index_ref[0]

    @pl.when(step == 0)
    def _():
        gains_ref[...] = jnp.zeros_like(gains_ref)
        for x in range(2):
            slot = device if x == 0 else 2 * group - 1 - device
            lane = lax.broadcasted_iota(jnp.int32, (block, block), 1)
            row = lax.broadcasted_iota(jnp.int32, (block, block), 0)
            query_position = slot * block + (lane if x == 0 else block - 1 - lane)
            for panel in range(PANELS):
                seen = slot - panel
                upward = seen < group
                key_position = (
                    seen * block
                    + jnp.where(upward, 0, block - 1)
                    + jnp.where(upward, 1, -1) * row
                )
                key_position = jnp.where(seen >= 0, key_position, -1)
                allowed = (doc_ref[x : x + 1, :] <= key_position) & (key_position <= query_position)
                value = jnp.where(allowed, 1.0, 0.0).astype(F32)
                for r in range(repeat):
                    mask_ref[
                        x, panel * block : (panel + 1) * block, r * block : (r + 1) * block
                    ] = value

    gain_q = jnp.broadcast_to(gain_q_ref[...] * query_factor, (block, width))
    gain_k = jnp.broadcast_to(gain_k_ref[...], (block, width))
    even = device % 2 == 0
    at_fold = device == group - 1
    near, far = [], []
    for part, own_ref in ((0, k_ref), (1, v_ref)):
        from_pair, from_cross = pair_ref[part], cross_ref[part]
        from_skip, from_relay = skip_ref[part], relay_ref[part]
        high_near = jnp.where(even, from_pair, jnp.where(at_fold, own_ref[0], from_cross))
        high_far = jnp.where(even, from_relay, jnp.where(at_fold, from_pair, from_skip))
        near.append((jnp.where(even, from_cross, from_pair), high_near))
        far.append((jnp.where(even, from_skip, from_relay), high_far))
    near_grad, far_grad = [], []
    halves = range(2)
    sides = range(repeat)
    spans = range(PANELS)
    cols = [slice(r * width, (r + 1) * width) for r in sides]
    raw_q = [[q_ref[x, :, cols[r]] for r in sides] for x in halves]
    raw_k = [(k_ref[x], near[0][x], far[0][x]) for x in halves]
    k_norm = [
        [(raw_k[x][0].astype(F32) * ki_ref[x], ki_ref[x])]
        + [normalize(raw_k[x][p].astype(F32)) for p in spans[1:]]
        for x in halves
    ]
    q_rot = [jnp.concatenate([qr_ref[x, :, cols[r]] for r in sides], axis=0) for x in halves]
    k_rot = [
        jnp.concatenate(
            [kr_ref[x]]
            + [
                rotate(raw_k[x][p], k_norm[x][p][1], gain_k, cos_ref[x, p], sin_ref[x, p]).astype(BF16)
                for p in spans[1:]
            ],
            axis=0,
        )
        for x in halves
    ]
    cot = [jnp.concatenate([c_ref[x, :, cols[r]] for r in sides], axis=0) for x in halves]
    vals = [jnp.concatenate([v_ref[x], near[1][x], far[1][x]], axis=0) for x in halves]
    score = [contract(k_rot[x], q_rot[x], 1, 1) for x in halves]
    dprob = [contract(vals[x], cot[x], 1, 1) for x in halves]
    probs, dscore = [], []
    for x in halves:
        expo = jnp.exp(score[x]) * mask_ref[x]
        prob = expo * (1.0 / jnp.sum(expo, axis=0, keepdims=True))
        delta = jnp.sum(prob * dprob[x], axis=0, keepdims=True)
        dscore.append((prob * (dprob[x] - delta)).astype(BF16))
        probs.append(prob.astype(BF16))
    grad_v = [contract(probs[x], cot[x], 1, 0) for x in halves]
    grad_k = [contract(dscore[x], q_rot[x], 1, 0) for x in halves]
    grad_q = [contract(dscore[x], k_rot[x], 0, 0) for x in halves]
    attended = [contract(probs[x], vals[x], 0, 0) for x in halves]
    sum_q = jnp.zeros((1, width), F32)
    sum_k = jnp.zeros((1, width), F32)
    for x in halves:
        for p in spans:
            rows = slice(p * block, (p + 1) * block)
            normed, inverse = k_norm[x][p]
            back = unrotate(grad_k[x][rows], cos_ref[x, p], sin_ref[x, p])
            sum_k = sum_k + jnp.sum(back * normed, axis=0, keepdims=True)
            raw = norm_back(back * gain_k, normed, inverse)
            if p == 0:
                own_k_ref[x] = raw
                own_v_ref[x] = grad_v[x][rows]
            else:
                target = near_grad if p == 1 else far_grad
                target.append((raw, grad_v[x][rows]))
        for r in sides:
            rows = slice(r * block, (r + 1) * block)
            inverse = qi_ref[x, :, cols[r]]
            normed = raw_q[x][r].astype(F32) * inverse
            back = unrotate(grad_q[x][rows], cos_ref[x, 0], sin_ref[x, 0])
            sum_q = sum_q + jnp.sum(back * normed, axis=0, keepdims=True)
            gq_ref[x, :, cols[r]] = norm_back(back * gain_q, normed, inverse).astype(BF16)
            att_ref[x, :, cols[r]] = attended[x][rows].astype(BF16)
    for part in range(2):
        low, high = near_grad[0][part], near_grad[1][part]
        low_far, high_far = far_grad[0][part], far_grad[1][part]
        joined = jnp.where(at_fold, low + high_far, low)
        near_pair_out[part] = jnp.where(even, high, joined).astype(BF16)
        near_cross_out[part] = jnp.where(even, low, high).astype(BF16)
        far_pair_out[part] = jnp.where(even, high_far, low_far).astype(BF16)
        far_cross_out[part] = jnp.where(even, low_far, high_far).astype(BF16)
    gains_ref[0:1, :] += sum_q * query_factor
    gains_ref[1:2, :] += sum_k


def attend(group, device, doc_start, gain_q, gain_k, cosine, sine, queries, keys, values, cotangent, panels, prepared):
    block = queries.shape[1]
    width = gain_q.shape[0]
    heads = keys.shape[2] // width
    repeat = queries.shape[2] // keys.shape[2]
    whole = lambda shape: pl.BlockSpec(shape, lambda h: (0,) * len(shape))
    wide = pl.BlockSpec((2, block, repeat * width), lambda h: (0, 0, h))
    slim = pl.BlockSpec((2, block, width), lambda h: (0, 0, h))
    pair = jax.ShapeDtypeStruct((2, block, heads * width), BF16)
    pairs = 2 * heads * block * repeat * block * PANELS * width
    return pl.pallas_call(
        functools.partial(attend_kernel, group),
        grid=(heads,),
        in_specs=[
            pl.BlockSpec(memory_space=pltpu.SMEM),
            whole((2, block)),
            whole((1, width)),
            whole((1, width)),
            whole((2, PANELS, block, width)),
            whole((2, PANELS, block, width)),
            wide,
            slim,
            slim,
            wide,
            slim,
            slim,
            slim,
            slim,
            wide,
            wide,
            slim,
            slim,
        ],
        out_specs=[wide, wide, slim, slim, slim, slim, slim, slim, whole((2, width))],
        out_shape=[
            pltpu.HBM(queries.shape, BF16),
            pltpu.HBM(queries.shape, BF16),
            pltpu.HBM(keys.shape, F32),
            pltpu.HBM(keys.shape, F32),
            pair,
            pair,
            pair,
            pair,
            jax.ShapeDtypeStruct((2, width), F32),
        ],
        scratch_shapes=[pltpu.VMEM((2, PANELS * block, repeat * block), F32)],
        compiler_params=pltpu.CompilerParams(
            dimension_semantics=("arbitrary",), vmem_limit_bytes=32 * 1024 * 1024
        ),
        cost_estimate=pl.CostEstimate(
            flops=12 * pairs, bytes_accessed=12 * 1024 * 1024, transcendentals=pairs // width
        ),
        name="attend",
    )(device, doc_start, gain_q[None], gain_k[None], cosine, sine, *map(in_hbm, (queries, keys, values, cotangent)), *panels, *map(in_hbm, prepared))


def gather_kernel(group, index_ref, own_k_ref, own_v_ref, cross_ref, skip_ref, pair_ref, pay_ref, gk_ref, gv_ref):
    device = index_ref[0]
    even = device % 2 == 0
    at_fold = device == group - 1
    tile = own_k_ref.shape[1]
    rows = pl.ds(pl.multiple_of(pl.program_id(0) * tile, tile), tile)
    for part, own_ref, out_ref in ((0, own_k_ref, gk_ref), (1, own_v_ref, gv_ref)):
        direct = pair_ref[part, rows].astype(F32) + skip_ref[part, rows].astype(F32)
        across = cross_ref[part, rows].astype(F32)
        across = across + jnp.where(at_fold, pay_ref[part, rows].astype(F32), 0.0)
        out_ref[0] = (own_ref[0] + jnp.where(even, direct, across)).astype(BF16)
        out_ref[1] = (own_ref[1] + jnp.where(even, across, direct)).astype(BF16)


def gather(group, device, own_k, own_v, *arrived):
    _, block, columns = own_k.shape
    tile = block // 4
    spec = pl.BlockSpec((2, tile, columns), lambda h: (0, h, 0))
    return pl.pallas_call(
        functools.partial(gather_kernel, group),
        grid=(block // tile,),
        in_specs=[pl.BlockSpec(memory_space=pltpu.SMEM)]
        + [spec] * 2
        + [pl.BlockSpec(memory_space=pltpu.VMEM)] * 4,
        out_specs=[spec, spec],
        out_shape=[pltpu.HBM(own_k.shape, BF16)] * 2,
        compiler_params=pltpu.CompilerParams(
            dimension_semantics=("arbitrary",), vmem_limit_bytes=32 * 1024 * 1024
        ),
        cost_estimate=pl.CostEstimate(
            flops=8 * own_k.size, bytes_accessed=16 * own_k.size, transcendentals=0
        ),
        name="gather",
    )(device, in_hbm(own_k), in_hbm(own_v), *arrived)


def move(x, pairs):
    return lax.ppermute(x, "ctx", pairs)


def total_over(x, axis, first, last):
    size = lax.axis_size(axis)
    distance = first
    while distance < last:
        x = x + lax.ppermute(x, axis, [(i, i ^ distance) for i in range(size)])
        distance *= 2
    return x


def shards(queries, keys, values, doc_start, gain_q, key_norm_gain, cotangent):
    group = lax.axis_size("ctx")
    block = queries.shape[1]
    width = gain_q.shape[0]
    device = lax.axis_index("ctx")
    index = device[None].astype(jnp.int32)
    even = device % 2 == 0
    at_fold = device == group - 1
    evens = range(0, group, 2)
    pairs = [(i, i ^ 1) for i in range(group)]
    cross = [(i + 1, i + 2) for i in evens if i + 2 < group]
    cross = cross + [(b, a) for a, b in cross]
    skip_in = [(i, i + 2) for i in evens if i + 2 < group]
    skip_in = skip_in + [(i + 3, i + 1) for i in evens if i + 3 < group]
    skip_out = [(b, a) for a, b in skip_in]

    low = jnp.stack([keys[0], values[0]])
    high = jnp.stack([keys[1], values[1]])
    first = jnp.where(even, low, high)
    second = jnp.where(even, high, low)
    from_cross = move(second, cross)
    from_skip = move(first, skip_in)
    from_pair = move(first, pairs)

    rows = jnp.arange(block, dtype=jnp.int32)
    slots = jnp.stack([device, 2 * group - 1 - device])[:, None] - jnp.arange(PANELS)[None, :]
    angle = rotary_angles(slot_positions(slots[..., None], rows, group, block), width)
    cosine = jnp.cos(angle)
    sine = jnp.sin(angle)
    cosine = jnp.concatenate([cosine, cosine], axis=-1)
    sine = jnp.concatenate([-sine, sine], axis=-1)
    prepared = prepare(gain_q, key_norm_gain, cosine[:, 0], sine[:, 0], queries, keys)
    from_cross, *prepared = lax.optimization_barrier((from_cross, *prepared))
    from_relay = move(jnp.where(at_fold, second, from_cross), pairs)

    attended, grad_queries, own_k, own_v, near_pair, near_cross, far_pair, far_cross, gains = attend(
        group,
        index,
        doc_start,
        gain_q,
        key_norm_gain,
        cosine,
        sine,
        queries,
        keys,
        values,
        cotangent,
        (from_pair, from_cross, from_skip, from_relay),
        prepared,
    )
    back_relay = move(far_pair, pairs)
    pay = (near_cross.astype(F32) + back_relay.astype(F32)).astype(BF16)
    near_pair, far_cross, pay = lax.optimization_barrier((near_pair, far_cross, pay))
    back_cross = move(pay, cross)
    back_skip = move(far_cross, skip_out)
    back_pair = move(near_pair, pairs)
    everyone = lax.axis_size("ctx") * lax.axis_size("dp")
    spread = jnp.broadcast_to(gains[None], (everyone,) + gains.shape)
    gains = jnp.sum(lax.all_to_all(spread, ("dp", "ctx"), 0, 0, tiled=True), axis=0)
    grad_keys, grad_values = gather(group, index, own_k, own_v, back_cross, back_skip, back_pair, pay)
    return attended, grad_queries, grad_keys, grad_values, gains[0], gains[1]


def solution(mesh):
    tokens = P(None, ("dp", "ctx"), None)
    return jax.shard_map(
        shards,
        mesh=mesh,
        in_specs=(tokens, tokens, tokens, P(None, ("dp", "ctx")), P(), P(), tokens),
        out_specs=(tokens, tokens, tokens, tokens, P(), P()),
        check_vma=False,
    )
```

```python
import functools

import jax
import jax.numpy as jnp
from jax import lax
from jax.experimental import pallas as pl
from jax.experimental.pallas import tpu as pltpu
from jax.sharding import PartitionSpec as P

query_factor = 168.0 ** (-0.5)
rotary_base = 1000000.0
norm_epsilon = 1e-06
PANELS = 3
F32 = jnp.float32
BF16 = jnp.bfloat16


def rotary_angles(position, head_width):
    exponent = jnp.arange(head_width // 2, dtype=F32) * (2.0 / head_width)
    frequency = jnp.exp(-exponent * jnp.log(F32(rotary_base)))
    return position.astype(F32)[..., None] * frequency


def slot_positions(slot, rows, group, block):
    ascending = slot * block + rows
    descending = slot * block + block - 1 - rows
    inside = (slot >= 0) & (slot < 2 * group)
    return jnp.where(inside, jnp.where(slot < group, ascending, descending), -1)


def half_turn(x):
    return pltpu.roll(x, x.shape[-1] // 2, 1)


def lane_sum(x, terms):
    width = x.shape[-1]
    parts = []
    for _ in range(terms):
        parts.append(x.astype(BF16))
        x = x - parts[-1].astype(F32)
    split = jnp.concatenate(parts, axis=-1)
    return contract(split, jnp.ones((terms * width, width), BF16), 1, 0)


def normalize(x):
    inverse = lax.rsqrt(lane_sum(x * x, 2) * (1.0 / x.shape[-1]) + norm_epsilon)
    return x * inverse, inverse


def rotate(raw, inverse, gain, cosine, sine):
    turned = half_turn(raw).astype(F32)
    return inverse * (raw.astype(F32) * (gain * cosine) + turned * (half_turn(gain) * sine))


def unrotate(g, cosine, sine):
    return g * cosine + half_turn(g * sine)


def norm_back(grad, normed, inverse):
    return inverse * (grad - normed * (lane_sum(grad * normed, 1) * (1.0 / grad.shape[-1])))


def contract(a, b, da, db):
    return lax.dot_general(a, b, (((da,), (db,)), ((), ())), preferred_element_type=F32)


def in_hbm(x):
    return pltpu.with_memory_space_constraint(x, pltpu.HBM)


def prepare_kernel(gain_q_ref, gain_k_ref, cos_ref, sin_ref, q_ref, k_ref, qr_ref, qi_ref, kr_ref, ki_ref):
    width = gain_q_ref.shape[1]
    jobs = []
    for x in range(2):
        jobs.append((x, k_ref, kr_ref, ki_ref, slice(0, width), gain_k_ref[...]))
        for r in range(q_ref.shape[2] // width):
            cols = slice(r * width, (r + 1) * width)
            jobs.append((x, q_ref, qr_ref, qi_ref, cols, gain_q_ref[...] * query_factor))
    norms = [normalize(src[x, :, cols].astype(F32))[1] for x, src, _, _, cols, _ in jobs]
    for inverse, (x, src, out, inv_out, cols, gain) in zip(norms, jobs):
        gain = jnp.broadcast_to(gain, inverse.shape)
        turned = rotate(src[x, :, cols], inverse, gain, cos_ref[x], sin_ref[x])
        out[x, :, cols] = turned.astype(BF16)
        inv_out[x, :, cols] = inverse


def prepare(gain_q, gain_k, cosine, sine, queries, keys):
    _, block, columns = keys.shape
    width = gain_q.shape[0]
    repeat = queries.shape[2] // columns
    whole = lambda shape: pl.BlockSpec(shape, lambda h: (0,) * len(shape))
    wide = pl.BlockSpec((2, block, repeat * width), lambda h: (0, 0, h))
    slim = pl.BlockSpec((2, block, width), lambda h: (0, 0, h))
    return pl.pallas_call(
        prepare_kernel,
        grid=(columns // width,),
        in_specs=[
            whole((1, width)),
            whole((1, width)),
            whole((2, block, width)),
            whole((2, block, width)),
            wide,
            slim,
        ],
        out_specs=[wide, wide, slim, slim],
        out_shape=[
            pltpu.HBM(queries.shape, BF16),
            pltpu.HBM(queries.shape, F32),
            pltpu.HBM(keys.shape, BF16),
            pltpu.HBM(keys.shape, F32),
        ],
        compiler_params=pltpu.CompilerParams(dimension_semantics=("arbitrary",)),
        cost_estimate=pl.CostEstimate(
            flops=64 * queries.size, bytes_accessed=16 * queries.size, transcendentals=queries.size
        ),
        name="prepare",
    )(gain_q[None], gain_k[None], cosine, sine, in_hbm(queries), in_hbm(keys))


def attend_kernel(
    group,
    index_ref,
    doc_ref,
    gain_q_ref,
    gain_k_ref,
    cos_ref,
    sin_ref,
    q_ref,
    k_ref,
    v_ref,
    c_ref,
    pair_ref,
    cross_ref,
    skip_ref,
    relay_ref,
    qr_ref,
    qi_ref,
    kr_ref,
    ki_ref,
    att_ref,
    gq_ref,
    own_k_ref,
    own_v_ref,
    near_pair_out,
    near_cross_out,
    far_pair_out,
    far_cross_out,
    gains_ref,
    mask_ref,
):
    step = pl.program_id(0)
    block = q_ref.shape[1]
    width = k_ref.shape[2]
    repeat = q_ref.shape[2] // width
    device = index_ref[0]

    @pl.when(step == 0)
    def _():
        gains_ref[...] = jnp.zeros_like(gains_ref)
        for x in range(2):
            slot = device if x == 0 else 2 * group - 1 - device
            lane = lax.broadcasted_iota(jnp.int32, (block, block), 1)
            row = lax.broadcasted_iota(jnp.int32, (block, block), 0)
            query_position = slot * block + (lane if x == 0 else block - 1 - lane)
            for panel in range(PANELS):
                seen = slot - panel
                upward = seen < group
                key_position = (
                    seen * block
                    + jnp.where(upward, 0, block - 1)
                    + jnp.where(upward, 1, -1) * row
                )
                key_position = jnp.where(seen >= 0, key_position, -1)
                allowed = (doc_ref[x : x + 1, :] <= key_position) & (key_position <= query_position)
                value = jnp.where(allowed, 1.0, 0.0).astype(F32)
                for r in range(repeat):
                    mask_ref[
                        x, panel * block : (panel + 1) * block, r * block : (r + 1) * block
                    ] = value

    gain_q = jnp.broadcast_to(gain_q_ref[...] * query_factor, (block, width))
    gain_k = jnp.broadcast_to(gain_k_ref[...], (block, width))
    even = device % 2 == 0
    at_fold = device == group - 1
    near, far = [], []
    for part, own_ref in ((0, k_ref), (1, v_ref)):
        from_pair, from_cross = pair_ref[part], cross_ref[part]
        from_skip, from_relay = skip_ref[part], relay_ref[part]
        high_near = jnp.where(even, from_pair, jnp.where(at_fold, own_ref[0], from_cross))
        high_far = jnp.where(even, from_relay, jnp.where(at_fold, from_pair, from_skip))
        near.append((jnp.where(even, from_cross, from_pair), high_near))
        far.append((jnp.where(even, from_skip, from_relay), high_far))
    near_grad, far_grad = [], []
    halves = range(2)
    sides = range(repeat)
    spans = range(PANELS)
    cols = [slice(r * width, (r + 1) * width) for r in sides]
    raw_q = [[q_ref[x, :, cols[r]] for r in sides] for x in halves]
    raw_k = [(k_ref[x], near[0][x], far[0][x]) for x in halves]
    k_norm = [
        [(raw_k[x][0].astype(F32) * ki_ref[x], ki_ref[x])]
        + [normalize(raw_k[x][p].astype(F32)) for p in spans[1:]]
        for x in halves
    ]
    q_rot = [jnp.concatenate([qr_ref[x, :, cols[r]] for r in sides], axis=0) for x in halves]
    k_rot = [
        jnp.concatenate(
            [kr_ref[x]]
            + [
                rotate(raw_k[x][p], k_norm[x][p][1], gain_k, cos_ref[x, p], sin_ref[x, p]).astype(BF16)
                for p in spans[1:]
            ],
            axis=0,
        )
        for x in halves
    ]
    cot = [jnp.concatenate([c_ref[x, :, cols[r]] for r in sides], axis=0) for x in halves]
    vals = [jnp.concatenate([v_ref[x], near[1][x], far[1][x]], axis=0) for x in halves]
    score = [contract(k_rot[x], q_rot[x], 1, 1) for x in halves]
    dprob = [contract(vals[x], cot[x], 1, 1) for x in halves]
    probs, dscore = [], []
    for x in halves:
        expo = jnp.exp(score[x]) * mask_ref[x]
        prob = expo * (1.0 / jnp.sum(expo, axis=0, keepdims=True))
        delta = jnp.sum(prob * dprob[x], axis=0, keepdims=True)
        dscore.append((prob * (dprob[x] - delta)).astype(BF16))
        probs.append(prob.astype(BF16))
    grad_v = [contract(probs[x], cot[x], 1, 0) for x in halves]
    grad_k = [contract(dscore[x], q_rot[x], 1, 0) for x in halves]
    grad_q = [contract(dscore[x], k_rot[x], 0, 0) for x in halves]
    attended = [contract(probs[x], vals[x], 0, 0) for x in halves]
    sum_q = jnp.zeros((1, width), F32)
    sum_k = jnp.zeros((1, width), F32)
    for x in halves:
        for p in spans:
            rows = slice(p * block, (p + 1) * block)
            normed, inverse = k_norm[x][p]
            back = unrotate(grad_k[x][rows], cos_ref[x, p], sin_ref[x, p])
            sum_k = sum_k + jnp.sum(back * normed, axis=0, keepdims=True)
            raw = norm_back(back * gain_k, normed, inverse)
            if p == 0:
                own_k_ref[x] = raw
                own_v_ref[x] = grad_v[x][rows]
            else:
                target = near_grad if p == 1 else far_grad
                target.append((raw, grad_v[x][rows]))
        for r in sides:
            rows = slice(r * block, (r + 1) * block)
            inverse = qi_ref[x, :, cols[r]]
            normed = raw_q[x][r].astype(F32) * inverse
            back = unrotate(grad_q[x][rows], cos_ref[x, 0], sin_ref[x, 0])
            sum_q = sum_q + jnp.sum(back * normed, axis=0, keepdims=True)
            gq_ref[x, :, cols[r]] = norm_back(back * gain_q, normed, inverse).astype(BF16)
            att_ref[x, :, cols[r]] = attended[x][rows].astype(BF16)
    for part in range(2):
        low, high = near_grad[0][part], near_grad[1][part]
        low_far, high_far = far_grad[0][part], far_grad[1][part]
        joined = jnp.where(at_fold, low + high_far, low)
        near_pair_out[part] = jnp.where(even, high, joined).astype(BF16)
        near_cross_out[part] = jnp.where(even, low, high).astype(BF16)
        far_pair_out[part] = jnp.where(even, high_far, low_far).astype(BF16)
        far_cross_out[part] = jnp.where(even, low_far, high_far).astype(BF16)
    gains_ref[0:1, :] += sum_q * query_factor
    gains_ref[1:2, :] += sum_k


def attend(group, device, doc_start, gain_q, gain_k, cosine, sine, queries, keys, values, cotangent, panels, prepared):
    block = queries.shape[1]
    width = gain_q.shape[0]
    heads = keys.shape[2] // width
    repeat = queries.shape[2] // keys.shape[2]
    whole = lambda shape: pl.BlockSpec(shape, lambda h: (0,) * len(shape))
    wide = pl.BlockSpec((2, block, repeat * width), lambda h: (0, 0, h))
    slim = pl.BlockSpec((2, block, width), lambda h: (0, 0, h))
    pair = jax.ShapeDtypeStruct((2, block, heads * width), BF16)
    pairs = 2 * heads * block * repeat * block * PANELS * width
    return pl.pallas_call(
        functools.partial(attend_kernel, group),
        grid=(heads,),
        in_specs=[
            pl.BlockSpec(memory_space=pltpu.SMEM),
            whole((2, block)),
            whole((1, width)),
            whole((1, width)),
            whole((2, PANELS, block, width)),
            whole((2, PANELS, block, width)),
            wide,
            slim,
            slim,
            wide,
            slim,
            slim,
            slim,
            slim,
            wide,
            wide,
            slim,
            slim,
        ],
        out_specs=[wide, wide, slim, slim, slim, slim, slim, slim, whole((2, width))],
        out_shape=[
            pltpu.HBM(queries.shape, BF16),
            pltpu.HBM(queries.shape, BF16),
            pltpu.HBM(keys.shape, F32),
            pltpu.HBM(keys.shape, F32),
            pair,
            pair,
            pair,
            pair,
            jax.ShapeDtypeStruct((2, width), F32),
        ],
        scratch_shapes=[pltpu.VMEM((2, PANELS * block, repeat * block), F32)],
        compiler_params=pltpu.CompilerParams(
            dimension_semantics=("arbitrary",), vmem_limit_bytes=32 * 1024 * 1024
        ),
        cost_estimate=pl.CostEstimate(
            flops=12 * pairs, bytes_accessed=12 * 1024 * 1024, transcendentals=pairs // width
        ),
        name="attend",
    )(device, doc_start, gain_q[None], gain_k[None], cosine, sine, *map(in_hbm, (queries, keys, values, cotangent)), *panels, *map(in_hbm, prepared))


def gather_kernel(index_ref, own_k_ref, own_v_ref, cross_ref, skip_ref, pair_ref, gk_ref, gv_ref):
    device = index_ref[0]
    even = device % 2 == 0
    tile = own_k_ref.shape[1]
    rows = pl.ds(pl.multiple_of(pl.program_id(0) * tile, tile), tile)
    for part, own_ref, out_ref in ((0, own_k_ref, gk_ref), (1, own_v_ref, gv_ref)):
        direct = pair_ref[part, rows].astype(F32) + skip_ref[part, rows].astype(F32)
        across = cross_ref[part, rows]
        out_ref[0] = (own_ref[0] + jnp.where(even, direct, across)).astype(BF16)
        out_ref[1] = (own_ref[1] + jnp.where(even, across, direct)).astype(BF16)


def gather(device, own_k, own_v, *arrived):
    _, block, columns = own_k.shape
    tile = block // 2
    spec = pl.BlockSpec((2, tile, columns), lambda h: (0, h, 0))
    return pl.pallas_call(
        gather_kernel,
        grid=(block // tile,),
        in_specs=[pl.BlockSpec(memory_space=pltpu.SMEM)]
        + [spec] * 2
        + [pl.BlockSpec(memory_space=pltpu.VMEM)] * 3,
        out_specs=[spec, spec],
        out_shape=[pltpu.HBM(own_k.shape, BF16)] * 2,
        compiler_params=pltpu.CompilerParams(
            dimension_semantics=("arbitrary",), vmem_limit_bytes=32 * 1024 * 1024
        ),
        cost_estimate=pl.CostEstimate(
            flops=8 * own_k.size, bytes_accessed=16 * own_k.size, transcendentals=0
        ),
        name="gather",
    )(device, in_hbm(own_k), in_hbm(own_v), *arrived)


def move(x, pairs):
    return lax.ppermute(x, "ctx", pairs)


def total_over(x, axis, first, last):
    size = lax.axis_size(axis)
    distance = first
    while distance < last:
        x = x + lax.ppermute(x, axis, [(i, i ^ distance) for i in range(size)])
        distance *= 2
    return x


def shards(queries, keys, values, doc_start, gain_q, key_norm_gain, cotangent):
    group = lax.axis_size("ctx")
    block = queries.shape[1]
    width = gain_q.shape[0]
    device = lax.axis_index("ctx")
    index = device[None].astype(jnp.int32)
    even = device % 2 == 0
    at_fold = device == group - 1
    evens = range(0, group, 2)
    pairs = [(i, i ^ 1) for i in range(group)]
    cross = [(i + 1, i + 2) for i in evens if i + 2 < group]
    cross = cross + [(b, a) for a, b in cross]
    skip_in = [(i, i + 2) for i in evens if i + 2 < group]
    skip_in = skip_in + [(i + 3, i + 1) for i in evens if i + 3 < group]
    skip_out = [(b, a) for a, b in skip_in]

    low = jnp.stack([keys[0], values[0]])
    high = jnp.stack([keys[1], values[1]])
    first = jnp.where(even, low, high)
    second = jnp.where(even, high, low)
    from_cross = move(second, cross)
    from_skip = move(first, skip_in)
    from_pair = move(first, pairs)

    rows = jnp.arange(block, dtype=jnp.int32)
    slots = jnp.stack([device, 2 * group - 1 - device])[:, None] - jnp.arange(PANELS)[None, :]
    angle = rotary_angles(slot_positions(slots[..., None], rows, group, block), width)
    cosine = jnp.cos(angle)
    sine = jnp.sin(angle)
    cosine = jnp.concatenate([cosine, cosine], axis=-1)
    sine = jnp.concatenate([-sine, sine], axis=-1)
    prepared = prepare(gain_q, key_norm_gain, cosine[:, 0], sine[:, 0], queries, keys)
    from_cross, *prepared = lax.optimization_barrier((from_cross, *prepared))
    from_relay = move(jnp.where(at_fold, second, from_cross), pairs)

    attended, grad_queries, own_k, own_v, near_pair, near_cross, far_pair, far_cross, gains = attend(
        group,
        index,
        doc_start,
        gain_q,
        key_norm_gain,
        cosine,
        sine,
        queries,
        keys,
        values,
        cotangent,
        (from_pair, from_cross, from_skip, from_relay),
        prepared,
    )
    back_relay = move(far_pair, pairs)
    pay = (near_cross.astype(F32) + back_relay.astype(F32)).astype(BF16)
    near_pair, far_cross, pay = lax.optimization_barrier((near_pair, far_cross, pay))
    back_cross = move(pay, cross)
    back_skip = move(far_cross, skip_out)
    back_pair = move(near_pair, pairs)
    everyone = lax.axis_size("ctx") * lax.axis_size("dp")
    spread = jnp.broadcast_to(gains[None], (everyone,) + gains.shape)
    gains = jnp.sum(lax.all_to_all(spread, ("dp", "ctx"), 0, 0, tiled=True), axis=0)
    across = back_cross.astype(F32) + jnp.where(at_fold, pay.astype(F32), 0.0)
    grad_keys, grad_values = gather(index, own_k, own_v, across, back_skip, back_pair)
    return attended, grad_queries, grad_keys, grad_values, gains[0], gains[1]


def solution(mesh):
    tokens = P(None, ("dp", "ctx"), None)
    return jax.shard_map(
        shards,
        mesh=mesh,
        in_specs=(tokens, tokens, tokens, P(None, ("dp", "ctx")), P(), P(), tokens),
        out_specs=(tokens, tokens, tokens, tokens, P(), P()),
        check_vma=False,
    )
```

```python
import functools

import jax
import jax.numpy as jnp
from jax import lax
from jax.experimental import pallas as pl
from jax.experimental.pallas import tpu as pltpu
from jax.sharding import PartitionSpec as P

query_factor = 168.0 ** (-0.5)
rotary_base = 1000000.0
norm_epsilon = 1e-06
PANELS = 3
F32 = jnp.float32
BF16 = jnp.bfloat16


def rotary_angles(position, head_width):
    exponent = jnp.arange(head_width // 2, dtype=F32) * (2.0 / head_width)
    frequency = jnp.exp(-exponent * jnp.log(F32(rotary_base)))
    return position.astype(F32)[..., None] * frequency


def slot_positions(slot, rows, group, block):
    ascending = slot * block + rows
    descending = slot * block + block - 1 - rows
    inside = (slot >= 0) & (slot < 2 * group)
    return jnp.where(inside, jnp.where(slot < group, ascending, descending), -1)


def half_turn(x):
    return pltpu.roll(x, x.shape[-1] // 2, 1)


def lane_sums(blocks, terms):
    size = blocks[0].shape[0]
    total = lane_sum(jnp.concatenate(blocks, axis=0), terms)
    return [total[i * size : (i + 1) * size] for i in range(len(blocks))]


def lane_sum(x, terms):
    width = x.shape[-1]
    parts = []
    for _ in range(terms):
        parts.append(x.astype(BF16))
        x = x - parts[-1].astype(F32)
    split = jnp.concatenate(parts, axis=-1)
    return contract(split, jnp.ones((terms * width, width), BF16), 1, 0)


def normalize(blocks):
    sums = lane_sums([x * x for x in blocks], 2)
    inverses = [lax.rsqrt(s * (1.0 / s.shape[-1]) + norm_epsilon) for s in sums]
    return [(x * inverse, inverse) for x, inverse in zip(blocks, inverses)]


def rotate(raw, inverse, gain, cosine, sine):
    turned = half_turn(raw).astype(F32)
    return inverse * (raw.astype(F32) * (gain * cosine) + turned * (half_turn(gain) * sine))


def unrotate(g, cosine, sine):
    return g * cosine + half_turn(g * sine)


def contract(a, b, da, db):
    return lax.dot_general(a, b, (((da,), (db,)), ((), ())), preferred_element_type=F32)


def in_hbm(x):
    return pltpu.with_memory_space_constraint(x, pltpu.HBM)


def prepare_kernel(gain_q_ref, gain_k_ref, cos_ref, sin_ref, q_ref, k_ref, qr_ref, qi_ref, kr_ref, ki_ref):
    width = gain_q_ref.shape[1]
    jobs = []
    for x in range(2):
        jobs.append((x, k_ref, kr_ref, ki_ref, slice(0, width), gain_k_ref[...]))
        for r in range(q_ref.shape[2] // width):
            cols = slice(r * width, (r + 1) * width)
            jobs.append((x, q_ref, qr_ref, qi_ref, cols, gain_q_ref[...] * query_factor))
    norms = normalize([src[x, :, cols].astype(F32) for x, src, _, _, cols, _ in jobs])
    for (_, inverse), (x, src, out, inv_out, cols, gain) in zip(norms, jobs):
        gain = jnp.broadcast_to(gain, inverse.shape)
        turned = rotate(src[x, :, cols], inverse, gain, cos_ref[x], sin_ref[x])
        out[x, :, cols] = turned.astype(BF16)
        inv_out[x, :, cols] = inverse


def prepare(gain_q, gain_k, cosine, sine, queries, keys):
    _, block, columns = keys.shape
    width = gain_q.shape[0]
    repeat = queries.shape[2] // columns
    whole = lambda shape: pl.BlockSpec(shape, lambda h: (0,) * len(shape))
    wide = pl.BlockSpec((2, block, repeat * width), lambda h: (0, 0, h))
    slim = pl.BlockSpec((2, block, width), lambda h: (0, 0, h))
    return pl.pallas_call(
        prepare_kernel,
        grid=(columns // width,),
        in_specs=[
            whole((1, width)),
            whole((1, width)),
            whole((2, block, width)),
            whole((2, block, width)),
            wide,
            slim,
        ],
        out_specs=[wide, wide, slim, slim],
        out_shape=[
            pltpu.HBM(queries.shape, BF16),
            pltpu.HBM(queries.shape, F32),
            pltpu.HBM(keys.shape, BF16),
            pltpu.HBM(keys.shape, F32),
        ],
        compiler_params=pltpu.CompilerParams(dimension_semantics=("arbitrary",)),
        cost_estimate=pl.CostEstimate(
            flops=64 * queries.size, bytes_accessed=16 * queries.size, transcendentals=queries.size
        ),
        name="prepare",
    )(gain_q[None], gain_k[None], cosine, sine, in_hbm(queries), in_hbm(keys))


def attend_kernel(
    group,
    index_ref,
    doc_ref,
    gain_q_ref,
    gain_k_ref,
    cos_ref,
    sin_ref,
    q_ref,
    k_ref,
    v_ref,
    c_ref,
    pair_ref,
    cross_ref,
    skip_ref,
    relay_ref,
    qr_ref,
    qi_ref,
    kr_ref,
    ki_ref,
    att_ref,
    gq_ref,
    own_k_ref,
    own_v_ref,
    near_pair_out,
    near_cross_out,
    far_pair_out,
    far_cross_out,
    gains_ref,
    mask_ref,
):
    step = pl.program_id(0)
    block = q_ref.shape[1]
    width = k_ref.shape[2]
    repeat = q_ref.shape[2] // width
    device = index_ref[0]

    @pl.when(step == 0)
    def _():
        gains_ref[...] = jnp.zeros_like(gains_ref)
        for x in range(2):
            slot = device if x == 0 else 2 * group - 1 - device
            lane = lax.broadcasted_iota(jnp.int32, (block, block), 1)
            row = lax.broadcasted_iota(jnp.int32, (block, block), 0)
            query_position = slot * block + (lane if x == 0 else block - 1 - lane)
            for panel in range(PANELS):
                seen = slot - panel
                upward = seen < group
                key_position = (
                    seen * block
                    + jnp.where(upward, 0, block - 1)
                    + jnp.where(upward, 1, -1) * row
                )
                key_position = jnp.where(seen >= 0, key_position, -1)
                allowed = (doc_ref[x : x + 1, :] <= key_position) & (key_position <= query_position)
                value = jnp.where(allowed, 1.0, 0.0).astype(F32)
                for r in range(repeat):
                    mask_ref[
                        x, panel * block : (panel + 1) * block, r * block : (r + 1) * block
                    ] = value

    gain_q = jnp.broadcast_to(gain_q_ref[...] * query_factor, (block, width))
    gain_k = jnp.broadcast_to(gain_k_ref[...], (block, width))
    even = device % 2 == 0
    at_fold = device == group - 1
    near, far = [], []
    for part, own_ref in ((0, k_ref), (1, v_ref)):
        from_pair, from_cross = pair_ref[part], cross_ref[part]
        from_skip, from_relay = skip_ref[part], relay_ref[part]
        high_near = jnp.where(even, from_pair, jnp.where(at_fold, own_ref[0], from_cross))
        high_far = jnp.where(even, from_relay, jnp.where(at_fold, from_pair, from_skip))
        near.append((jnp.where(even, from_cross, from_pair), high_near))
        far.append((jnp.where(even, from_skip, from_relay), high_far))
    near_grad, far_grad = [], []
    halves = range(2)
    sides = range(repeat)
    spans = range(PANELS)
    cols = [slice(r * width, (r + 1) * width) for r in sides]
    raw_q = [[q_ref[x, :, cols[r]] for r in sides] for x in halves]
    raw_k = [(k_ref[x], near[0][x], far[0][x]) for x in halves]
    arrived = normalize([raw_k[x][p].astype(F32) for x in halves for p in spans[1:]])
    k_norm = [
        [(raw_k[x][0].astype(F32) * ki_ref[x], ki_ref[x])]
        + arrived[x * (PANELS - 1) : (x + 1) * (PANELS - 1)]
        for x in halves
    ]
    q_rot = [jnp.concatenate([qr_ref[x, :, cols[r]] for r in sides], axis=0) for x in halves]
    k_rot = [
        jnp.concatenate(
            [kr_ref[x]]
            + [
                rotate(raw_k[x][p], k_norm[x][p][1], gain_k, cos_ref[x, p], sin_ref[x, p]).astype(BF16)
                for p in spans[1:]
            ],
            axis=0,
        )
        for x in halves
    ]
    cot = [jnp.concatenate([c_ref[x, :, cols[r]] for r in sides], axis=0) for x in halves]
    vals = [jnp.concatenate([v_ref[x], near[1][x], far[1][x]], axis=0) for x in halves]
    score = [contract(k_rot[x], q_rot[x], 1, 1) for x in halves]
    dprob = [contract(vals[x], cot[x], 1, 1) for x in halves]
    probs, dscore = [], []
    for x in halves:
        expo = jnp.exp(score[x]) * mask_ref[x]
        prob = expo * (1.0 / jnp.sum(expo, axis=0, keepdims=True))
        delta = jnp.sum(prob * dprob[x], axis=0, keepdims=True)
        dscore.append((prob * (dprob[x] - delta)).astype(BF16))
        probs.append(prob.astype(BF16))
    grad_v = [contract(probs[x], cot[x], 1, 0) for x in halves]
    grad_k = [contract(dscore[x], q_rot[x], 1, 0) for x in halves]
    grad_q = [contract(dscore[x], k_rot[x], 0, 0) for x in halves]
    attended = [contract(probs[x], vals[x], 0, 0) for x in halves]
    sum_q = jnp.zeros((1, width), F32)
    sum_k = jnp.zeros((1, width), F32)
    work = []
    for x in halves:
        for p in spans:
            rows = slice(p * block, (p + 1) * block)
            normed, inverse = k_norm[x][p]
            back = unrotate(grad_k[x][rows], cos_ref[x, p], sin_ref[x, p])
            sum_k = sum_k + jnp.sum(back * normed, axis=0, keepdims=True)
            work.append((back * gain_k, normed, inverse))
        for r in sides:
            rows = slice(r * block, (r + 1) * block)
            inverse = qi_ref[x, :, cols[r]]
            normed = raw_q[x][r].astype(F32) * inverse
            back = unrotate(grad_q[x][rows], cos_ref[x, 0], sin_ref[x, 0])
            sum_q = sum_q + jnp.sum(back * normed, axis=0, keepdims=True)
            work.append((back * gain_q, normed, inverse))
    means = lane_sums([grad * normed for grad, normed, _ in work], 1)
    done = [
        inverse * (grad - normed * (mean * (1.0 / width)))
        for (grad, normed, inverse), mean in zip(work, means)
    ]
    for x in halves:
        first = x * (PANELS + repeat)
        for p in spans:
            raw, value = done[first + p], grad_v[x][p * block : (p + 1) * block]
            if p == 0:
                own_k_ref[x] = raw
                own_v_ref[x] = value
            else:
                target = near_grad if p == 1 else far_grad
                target.append((raw, value))
        for r in sides:
            rows = slice(r * block, (r + 1) * block)
            gq_ref[x, :, cols[r]] = done[first + PANELS + r].astype(BF16)
            att_ref[x, :, cols[r]] = attended[x][rows].astype(BF16)
    for part in range(2):
        low, high = near_grad[0][part], near_grad[1][part]
        low_far, high_far = far_grad[0][part], far_grad[1][part]
        joined = jnp.where(at_fold, low + high_far, low)
        near_pair_out[part] = jnp.where(even, high, joined).astype(BF16)
        near_cross_out[part] = jnp.where(even, low, high).astype(BF16)
        far_pair_out[part] = jnp.where(even, high_far, low_far).astype(BF16)
        far_cross_out[part] = jnp.where(even, low_far, high_far).astype(BF16)
    gains_ref[0:1, :] += sum_q * query_factor
    gains_ref[1:2, :] += sum_k


def attend(group, device, doc_start, gain_q, gain_k, cosine, sine, queries, keys, values, cotangent, panels, prepared):
    block = queries.shape[1]
    width = gain_q.shape[0]
    heads = keys.shape[2] // width
    repeat = queries.shape[2] // keys.shape[2]
    whole = lambda shape: pl.BlockSpec(shape, lambda h: (0,) * len(shape))
    wide = pl.BlockSpec((2, block, repeat * width), lambda h: (0, 0, h))
    slim = pl.BlockSpec((2, block, width), lambda h: (0, 0, h))
    pair = jax.ShapeDtypeStruct((2, block, heads * width), BF16)
    pairs = 2 * heads * block * repeat * block * PANELS * width
    return pl.pallas_call(
        functools.partial(attend_kernel, group),
        grid=(heads,),
        in_specs=[
            pl.BlockSpec(memory_space=pltpu.SMEM),
            whole((2, block)),
            whole((1, width)),
            whole((1, width)),
            whole((2, PANELS, block, width)),
            whole((2, PANELS, block, width)),
            wide,
            slim,
            slim,
            wide,
            slim,
            slim,
            slim,
            slim,
            wide,
            wide,
            slim,
            slim,
        ],
        out_specs=[wide, wide, slim, slim, slim, slim, slim, slim, whole((2, width))],
        out_shape=[
            pltpu.HBM(queries.shape, BF16),
            pltpu.HBM(queries.shape, BF16),
            pltpu.HBM(keys.shape, F32),
            pltpu.HBM(keys.shape, F32),
            pair,
            pair,
            pair,
            pair,
            jax.ShapeDtypeStruct((2, width), F32),
        ],
        scratch_shapes=[pltpu.VMEM((2, PANELS * block, repeat * block), F32)],
        compiler_params=pltpu.CompilerParams(
            dimension_semantics=("arbitrary",), vmem_limit_bytes=32 * 1024 * 1024
        ),
        cost_estimate=pl.CostEstimate(
            flops=12 * pairs, bytes_accessed=12 * 1024 * 1024, transcendentals=pairs // width
        ),
        name="attend",
    )(device, doc_start, gain_q[None], gain_k[None], cosine, sine, *map(in_hbm, (queries, keys, values, cotangent)), *panels, *map(in_hbm, prepared))


def gather_kernel(index_ref, own_k_ref, own_v_ref, cross_ref, skip_ref, pair_ref, gk_ref, gv_ref):
    device = index_ref[0]
    even = device % 2 == 0
    tile = own_k_ref.shape[1]
    rows = pl.ds(pl.multiple_of(pl.program_id(0) * tile, tile), tile)
    for part, own_ref, out_ref in ((0, own_k_ref, gk_ref), (1, own_v_ref, gv_ref)):
        direct = pair_ref[part, rows].astype(F32) + skip_ref[part, rows].astype(F32)
        across = cross_ref[part, rows]
        out_ref[0] = (own_ref[0] + jnp.where(even, direct, across)).astype(BF16)
        out_ref[1] = (own_ref[1] + jnp.where(even, across, direct)).astype(BF16)


def gather(device, own_k, own_v, *arrived):
    _, block, columns = own_k.shape
    tile = block // 2
    spec = pl.BlockSpec((2, tile, columns), lambda h: (0, h, 0))
    return pl.pallas_call(
        gather_kernel,
        grid=(block // tile,),
        in_specs=[pl.BlockSpec(memory_space=pltpu.SMEM)]
        + [spec] * 2
        + [pl.BlockSpec(memory_space=pltpu.VMEM)] * 3,
        out_specs=[spec, spec],
        out_shape=[pltpu.HBM(own_k.shape, BF16)] * 2,
        compiler_params=pltpu.CompilerParams(
            dimension_semantics=("arbitrary",), vmem_limit_bytes=32 * 1024 * 1024
        ),
        cost_estimate=pl.CostEstimate(
            flops=8 * own_k.size, bytes_accessed=16 * own_k.size, transcendentals=0
        ),
        name="gather",
    )(device, in_hbm(own_k), in_hbm(own_v), *arrived)


def move(x, pairs):
    return lax.ppermute(x, "ctx", pairs)


def total_over(x, axis, first, last):
    size = lax.axis_size(axis)
    distance = first
    while distance < last:
        x = x + lax.ppermute(x, axis, [(i, i ^ distance) for i in range(size)])
        distance *= 2
    return x


def shards(queries, keys, values, doc_start, gain_q, key_norm_gain, cotangent):
    group = lax.axis_size("ctx")
    block = queries.shape[1]
    width = gain_q.shape[0]
    device = lax.axis_index("ctx")
    index = device[None].astype(jnp.int32)
    even = device % 2 == 0
    at_fold = device == group - 1
    evens = range(0, group, 2)
    pairs = [(i, i ^ 1) for i in range(group)]
    cross = [(i + 1, i + 2) for i in evens if i + 2 < group]
    cross = cross + [(b, a) for a, b in cross]
    skip_in = [(i, i + 2) for i in evens if i + 2 < group]
    skip_in = skip_in + [(i + 3, i + 1) for i in evens if i + 3 < group]
    skip_out = [(b, a) for a, b in skip_in]

    low = jnp.stack([keys[0], values[0]])
    high = jnp.stack([keys[1], values[1]])
    first = jnp.where(even, low, high)
    second = jnp.where(even, high, low)
    from_cross = move(second, cross)
    from_skip = move(first, skip_in)
    from_pair = move(first, pairs)

    rows = jnp.arange(block, dtype=jnp.int32)
    slots = jnp.stack([device, 2 * group - 1 - device])[:, None] - jnp.arange(PANELS)[None, :]
    angle = rotary_angles(slot_positions(slots[..., None], rows, group, block), width)
    cosine = jnp.cos(angle)
    sine = jnp.sin(angle)
    cosine = jnp.concatenate([cosine, cosine], axis=-1)
    sine = jnp.concatenate([-sine, sine], axis=-1)
    prepared = prepare(gain_q, key_norm_gain, cosine[:, 0], sine[:, 0], queries, keys)
    from_cross, *prepared = lax.optimization_barrier((from_cross, *prepared))
    from_relay = move(jnp.where(at_fold, second, from_cross), pairs)

    attended, grad_queries, own_k, own_v, near_pair, near_cross, far_pair, far_cross, gains = attend(
        group,
        index,
        doc_start,
        gain_q,
        key_norm_gain,
        cosine,
        sine,
        queries,
        keys,
        values,
        cotangent,
        (from_pair, from_cross, from_skip, from_relay),
        prepared,
    )
    back_relay = move(far_pair, pairs)
    pay = (near_cross.astype(F32) + back_relay.astype(F32)).astype(BF16)
    near_pair, far_cross, pay = lax.optimization_barrier((near_pair, far_cross, pay))
    back_cross = move(pay, cross)
    back_skip = move(far_cross, skip_out)
    back_pair = move(near_pair, pairs)
    everyone = lax.axis_size("ctx") * lax.axis_size("dp")
    spread = jnp.broadcast_to(gains[None], (everyone,) + gains.shape)
    gains = jnp.sum(lax.all_to_all(spread, ("dp", "ctx"), 0, 0, tiled=True), axis=0)
    across = back_cross.astype(F32) + jnp.where(at_fold, pay.astype(F32), 0.0)
    grad_keys, grad_values = gather(index, own_k, own_v, across, back_skip, back_pair)
    return attended, grad_queries, grad_keys, grad_values, gains[0], gains[1]


def solution(mesh):
    tokens = P(None, ("dp", "ctx"), None)
    return jax.shard_map(
        shards,
        mesh=mesh,
        in_specs=(tokens, tokens, tokens, P(None, ("dp", "ctx")), P(), P(), tokens),
        out_specs=(tokens, tokens, tokens, tokens, P(), P()),
        check_vma=False,
    )
```
